32 devices in a mesh: tok: 16 (over z, x, core), grp: 2 (over y).
Axes of the slice: x: 2, y: 2, z: 4, core: 2. Of those that a mesh axis runs over, the one named last changes fastest.
Arguments:
- tokens: bfloat16 [6144, 1024], P('tok', 'grp'), may hold values from -6 to 6
- cotangent: bfloat16 [6144, 1024], P('tok', 'grp'), may hold values from -6 to 6
- weights: bfloat16 [48, 5, 3, 128, 128], P('tok'), may hold values from -0.1875 to 0.1875
- pattern: int32 [48, 5, 3], P('tok'), may hold values from 0 to 2, all different within a row
- owners: int32 [720, 1], P('tok'), may hold values from 0 to 1; in each aligned block of 45 rows (0 to 44, 45 to 89, ...) at most 45 rows name the same one
- lat_in: bfloat16 [6144, 256], P('tok'), may hold values from -0.078125 to 0.078125
- lat_out: bfloat16 [6144, 256], P('tok'), may hold values from -0.375 to 0.375
Outputs:
- mixed: bfloat16 [6144, 1024], P('tok', 'grp')
- grad_tokens: bfloat16 [6144, 1024], P('tok', 'grp')
- grad_blocks: bfloat16 [1440, 128, 128], P(('tok', 'grp'))
The draws below stay inside these ranges and needn't reach their ends.
Inputs may be any that keep to these rules, and one draw needn't show every extreme that they name: `pattern`: each row names 3 different blocks of one device's tokens. `owners`: the 45 entries of one index of tok (aligned blocks) name each owner at most 45 times, a bound that some block reaches.
All inputs are finite; a program needn't handle non-finite values.
Results may differ from the reference program's by a relative error of at most 0.02.
Values may be sent and summed in bfloat16 or wider, within the bound.
No kernel may reach another device: no remote copies, remote signals or barrier semaphores. Data moves between devices by JAX's collectives and lax.ppermute only.
A program may use at most 64 MiB of HBM per device.

```python
import math
import jax
import jax.numpy as jnp
import numpy as np
from jax import lax

D = 1024
TOK_DEV = 384
BLK = 128
K = 3
R = 256
FACTORS = 5
TOKENS = 6144
C = 512
NRB = 48
NBLK = 45
NLIST = 720
MOST = 45
N_TOK = 16
N_GRP = 2


def block_levels(stream_key, shape, shards, least, top_value):
    gain = 1.0
    for axis_at, shards_of in shards:
        draws = jax.random.uniform(jax.random.fold_in(jax.random.fold_in(stream_key, 6), axis_at), (shards_of,), jnp.float32, least / len(shards), top_value / len(shards))
        gain = gain * jnp.repeat(jnp.exp(draws), shape[axis_at] // shards_of).reshape((-1,) + (1,) * (len(shape) - 1 - axis_at))
    return gain


def choose_distinct(rng, rows, count, top, lift):
    sequence = jax.random.permutation(jax.random.fold_in(rng, 1), count)
    favour = sequence
    for power in range(3):
        favour = favour * favour // count
    favour = favour * lift // count
    chance = jax.random.randint(jax.random.fold_in(rng, 2), (rows, count), 0, 4096) + favour
    fixed_rows = jax.random.permutation(jax.random.fold_in(rng, 3), rows)[jnp.arange(count) % rows]
    chance = jnp.where(jnp.arange(rows)[:, None] == fixed_rows[None, :], 1 << 14, chance)
    score = chance * count + jnp.arange(count)
    return lax.top_k(score.astype(jnp.int32), top)[1].astype(jnp.int32)


def assign_block(own_key, own, number, rows, count, top, limit, lean):
    ranking = jax.random.permutation(own_key, count)
    crowded, ordinary = load_shares(count, rows * top, limit, lean, True), load_shares(count, rows * top, limit, lean, False)
    places = jnp.arange(count)

    def named(lengths, turn):
        used = int((lengths > 0).sum())
        fixed = max(1, used // 4)
        passed = fixed + (places - fixed + turn * (used - fixed)) % max(1, count - fixed)
        return jnp.zeros((count,), jnp.int32).at[ranking[jnp.where(places < fixed, places, passed)]].set(jnp.asarray(lengths, jnp.int32))

    lengths = jnp.where(number % 4 == 0, named(crowded, number // 4), named(ordinary, number - number // 4 - 1))
    mixed = jax.random.permutation(jax.random.fold_in(own, 3), count)
    donor, receiver = mixed[0:count // 2 * 2:2], mixed[1:count // 2 * 2:2]
    room = jnp.minimum(lengths[donor] - 1, limit - lengths[receiver]) // 2
    room = jnp.where((donor == ranking[0]) | (receiver == ranking[0]) | (lengths[receiver] == 0), 0, jnp.maximum(room, 0))
    passed = jax.random.randint(jax.random.fold_in(own, 4), (count // 2,), 0, 1 << 20) % (room + 1)
    lengths = lengths.at[donor].add(-passed).at[receiver].add(passed)
    labels = jnp.searchsorted(jnp.cumsum(lengths), jnp.arange(rows * top), side="right").astype(jnp.int32)
    table = labels.reshape(top, rows).T
    table = table[jax.random.permutation(jax.random.fold_in(own, 1), rows)]
    turn = jax.random.randint(jax.random.fold_in(own, 2), (rows, 1), 0, top)
    return jnp.take_along_axis(table, (jnp.arange(top)[None, :] + turn) % top, axis=1)


def load_shares(number_of, total, bound, skew, full):
    portions = [(1 << 20) // math.isqrt(standing ** skew) + 1 for standing in range(1, number_of + 1)]
    largest = bound if full else min(bound, max(-(-total // number_of), total * portions[0] // sum(portions)))
    least = 1 if total - largest >= number_of - 1 else 0
    given, surplus = [largest] + [least] * (number_of - 1), total - largest - least * (number_of - 1)
    while surplus > 0:
        movable = [i for i in range(1, number_of) if given[i] < largest] or [i for i in range(1, number_of) if given[i] < bound]
        whole, budget = sum([portions[i] for i in movable]), surplus
        for i in movable:
            more = min(bound - given[i], max(1, budget * portions[i] // whole), surplus)
            given[i] = given[i] + more
            surplus = surplus - more
    return np.array(given)


def scatter_about(own_key, shape, deviation, limit, shards=(), kind=jnp.bfloat16):
    level = block_levels(own_key, shape, shards, -0.22, 0.18) if shards else 1.0
    entries = jax.random.normal(own_key, shape, jnp.float32) * deviation * level
    return jnp.minimum(jnp.maximum(entries, -limit), limit).astype(kind)


def setup_inputs(seed: int = 0) -> dict:
    key_list = jax.random.split(jax.random.key(seed), 8)
    tokens = scatter_about(key_list[0], (TOKENS, D), 1.0, 6.0, ((0, 16), (1, 2)))
    cotangent = scatter_about(key_list[1], (TOKENS, D), 1.0, 6.0, ((0, 16), (1, 2)))
    weights = scatter_about(key_list[2], (NRB, FACTORS, K, BLK, BLK), (3 * K * BLK) ** -0.5, 0.1875, ((0, 16),))
    pattern = choose_distinct(key_list[3], NRB * FACTORS, TOK_DEV // BLK, K, 0).reshape((NRB, FACTORS, K))
    owners_keys = jax.random.split(jax.random.fold_in(key_list[4], 1), NLIST // NBLK)
    owners_turns = jax.random.permutation(jax.random.fold_in(key_list[4], 3), NLIST // NBLK)
    owners = jax.vmap(lambda own, number: assign_block(jax.random.fold_in(key_list[4], 2), own, number, NBLK, N_GRP, 1, MOST, 2))(owners_keys, owners_turns).reshape((NLIST, 1))
    lat_in = scatter_about(key_list[5], (TOKENS, R), TOKENS ** -0.5, 0.078125, ((0, 16),))
    lat_out = scatter_about(key_list[6], (TOKENS, R), R ** -0.5, 0.375, ((0, 16),))
    return {"tokens": tokens, "cotangent": cotangent, "weights": weights, "pattern": pattern, "owners": owners, "lat_in": lat_in, "lat_out": lat_out}


def gelu_pair(z):
    act, back = jax.vjp(jax.nn.gelu, z)
    return (act, back(jnp.ones_like(z))[0])

def pick_all(source, picks):
    return jax.vmap(lambda src, pk: src[pk])(source, picks)

def reference(tokens, cotangent, weights, pattern, owners, lat_in, lat_out):
    f32 = jnp.float32
    bf16 = jnp.bfloat16
    nrb = TOK_DEV // BLK
    pat = pattern.reshape(N_TOK, nrb, FACTORS, K)
    wts = weights.reshape(N_TOK, nrb, FACTORS, K, BLK, BLK)
    current = tokens.reshape(N_TOK, nrb, BLK, D)
    sources = []
    zvalue = None
    for lev in range(FACTORS):
        if lev == 0:
            source = current
        else:
            source = current[np.arange(N_TOK) ^ 1 << lev - 1]
        sources.append(source)
        picked = pick_all(source, pat[:, :, lev])
        zvalue = current.astype(f32) + jnp.einsum('trkij,trkjc->tric', wts[:, :, lev].astype(f32), picked.astype(f32))
        if lev < FACTORS - 1:
            current = zvalue.astype(bf16)
    act, slope = gelu_pair(zvalue)
    lat_sum = jnp.dot(lat_in.T, tokens, preferred_element_type=f32)
    lat_grad = jnp.dot(lat_out.T, cotangent, preferred_element_type=f32)
    mixed = (act.reshape(TOKENS, D) + jnp.dot(lat_out, lat_sum.astype(bf16), preferred_element_type=f32)).astype(bf16)
    grad_z = (cotangent.reshape(N_TOK, nrb, BLK, D).astype(f32) * slope).astype(bf16)
    grads = [None] * FACTORS
    chain = None
    for lev in reversed(range(FACTORS)):
        picked = pick_all(sources[lev], pat[:, :, lev])
        dz_g = grad_z.reshape(N_TOK, nrb, BLK, N_GRP, C).astype(f32)
        pk_g = picked.reshape(N_TOK, nrb, K, BLK, N_GRP, C).astype(f32)
        partial_terms = jnp.einsum('trigc,trkjgc->trkgij', dz_g, pk_g).astype(bf16)
        partial_terms = lax.optimization_barrier(partial_terms)
        grads[lev] = lax.optimization_barrier(jnp.sum(partial_terms.astype(f32), axis=3))
        back = jnp.einsum('trkij,tric->trkjc', wts[:, :, lev].astype(f32), grad_z.astype(f32))
        onehot = (pat[:, :, lev][..., None] == jnp.arange(nrb, dtype=jnp.int32)).astype(f32)
        spread = jnp.einsum('trkb,trkjc->tbjc', onehot, back)
        if lev == 0:
            chain = grad_z.astype(f32) + spread
        else:
            incoming = spread.astype(bf16)[np.arange(N_TOK) ^ 1 << lev - 1]
            grad_z = (grad_z.astype(f32) + incoming.astype(f32)).astype(bf16)
    grad_tokens = (chain.reshape(TOKENS, D) + jnp.dot(lat_in, lat_grad.astype(bf16), preferred_element_type=f32)).astype(bf16)
    stacked = jnp.stack(grads, axis=2).reshape(N_TOK, NBLK, BLK, BLK).astype(bf16)
    own = owners.reshape(N_TOK, NBLK).astype(jnp.int32)
    marks = (own[..., None] == jnp.arange(N_GRP, dtype=jnp.int32)).astype(jnp.int32)
    ranks = jnp.cumsum(marks, axis=1) - marks
    slots = lax.optimization_barrier(jnp.sum(ranks * marks, axis=2)).astype(jnp.int32)
    tindex = jnp.broadcast_to(jnp.arange(N_TOK, dtype=jnp.int32)[:, None], (N_TOK, NBLK))
    placed = jnp.zeros((N_TOK, N_GRP, MOST, BLK, BLK), bf16).at[tindex, own, slots].set(stacked)
    grad_blocks = placed.reshape(N_TOK * N_GRP * MOST, BLK, BLK)
    return (mixed, grad_tokens, grad_blocks)
```

```python
import functools
import math
import jax
import jax.numpy as jnp
from jax import lax
from jax.experimental import pallas as pl
from jax.experimental.pallas import tpu as pltpu
from jax.sharding import PartitionSpec as P


F32 = jnp.float32
BF16 = jnp.bfloat16
CHUNKS = 2


def swapped(value, axis, stride):
    mask = 2**stride
    pairs = [(source, source ^ mask) for source in range(lax.axis_size(axis))]
    return lax.ppermute(value, axis, pairs)


def dot(a, b, dims=((1,), (0,))):
    return lax.dot_general(a, b, (dims, ((), ())), preferred_element_type=F32)


def source_of(pat, row, lev, block, count):
    where = jnp.int32(0)
    for k in range(1, count):
        where = jnp.where(pat[row, lev, k] == block, jnp.int32(k), where)
    return where


def row_weights(pat, w, row, lev, at, count):
    return jnp.concatenate(
        [w[row, at, source_of(pat, row, lev, j, count)] for j in range(count)], axis=1
    )


def back_product(pat, w, grad, lev, count, blk):
    out = []
    for j in range(count):
        column = jnp.concatenate(
            [w[r, 0, source_of(pat, r, lev, j, count)] for r in range(count)], axis=0
        )
        out.append(dot(column, grad, ((0,), (0,))))
    return out


def first_kernel(count, blk, width, pat, x, w, *outs):
    x_all = x[...]
    for r in range(count):
        z = x[r * blk : (r + 1) * blk, :].astype(F32) + dot(
            row_weights(pat, w, r, 0, 0, count), x_all
        )
        z = z.astype(BF16)
        for c, out in enumerate(outs):
            out[r * blk : (r + 1) * blk, :] = z[:, c * width : (c + 1) * width]


def forward_kernel(count, blk, lev, pat, y, src, w, out):
    src_all = src[...]
    for r in range(count):
        rows = slice(r * blk, (r + 1) * blk)
        z = y[rows, :].astype(F32) + dot(row_weights(pat, w, r, lev, 0, count), src_all)
        out[rows, :] = z.astype(BF16)


def turn_kernel(count, blk, lev, pat, y, src, cot, w, act, grad, back):
    src_all = src[...]
    scale = math.sqrt(2 / math.pi)
    for r in range(count):
        rows = slice(r * blk, (r + 1) * blk)
        z = y[rows, :].astype(F32) + dot(row_weights(pat, w, r, lev, 0, count), src_all)
        square = z * z
        t = jnp.tanh(scale * (z + 0.044715 * (square * z)))
        half = 0.5 * z
        cdf = 0.5 + 0.5 * t
        act[rows, :] = z * cdf
        slope = cdf + (half * (1.0 - t * t)) * (scale + (3 * 0.044715 * scale) * square)
        grad[rows, :] = (cot[rows, :].astype(F32) * slope).astype(BF16)
    for j, term in enumerate(back_product(pat, w, grad[...], lev, count, blk)):
        back[j * blk : (j + 1) * blk, :] = term.astype(BF16)


def backward_kernel(count, blk, lev, pat, old, term_in, w, grad, back):
    grad[...] = (old[...].astype(F32) + term_in[...].astype(F32)).astype(BF16)
    for j, term in enumerate(back_product(pat, w, grad[...], lev, count, blk)):
        back[j * blk : (j + 1) * blk, :] = term.astype(BF16)


def base_kernel(count, blk, pat, old, term_in, w, grad, chain):
    total = old[...].astype(F32) + term_in[...].astype(F32)
    grad[...] = total.astype(BF16)
    for j, term in enumerate(back_product(pat, w, grad[...], 0, count, blk)):
        rows = slice(j * blk, (j + 1) * blk)
        chain[rows, :] = grad[rows, :].astype(F32) + term


def weight_kernel(count, blk, lev, parts, pat, *refs):
    grads, sources, out = refs[:parts], refs[parts:-1], refs[-1]
    for r in range(count):
        rows = slice(r * blk, (r + 1) * blk)
        total = None
        for grad, source in zip(grads, sources):
            term = dot(grad[rows, :], source[...], ((1,), (1,)))
            total = term if total is None else total + term
        total = total.astype(BF16)
        for j in range(count):
            k = source_of(pat, r, lev, j, count)
            out[r * count + k] = total[:, j * blk : (j + 1) * blk]


def latent_kernel(width, parts, lat, small, *refs):
    acts, out = refs[:-1], refs[-1]
    for c in range(parts):
        cols = slice(c * width, (c + 1) * width)
        out[:, cols] = (acts[c][...] + dot(lat[...], small[:, cols])).astype(BF16)


def place_kernel(count, levels, own, mine, *refs):
    parts, out = refs[:-1], refs[-1]
    here, there = parts[:levels], parts[levels:]
    me = mine[0]
    out[...] = jnp.zeros_like(out)
    slot = jnp.int32(0)
    for r in range(count):
        for lev in range(levels):
            for k in range(count):
                i = (r * levels + lev) * count + k
                at = r * count + k
                owned = own[i, 0] == me

                @pl.when(owned)
                def _(lev=lev, at=at, slot=slot):
                    out[slot] = (
                        here[lev][at].astype(F32) + there[lev][at].astype(F32)
                    ).astype(BF16)

                slot = slot + owned.astype(jnp.int32)


def call(kernel, outs, name, flops, moved, *args):
    smem = pl.BlockSpec(memory_space=pltpu.SMEM)
    specs = []
    values = []
    for arg in args:
        if isinstance(arg, tuple):
            values.append(arg[0])
            specs.append(arg[1])
        else:
            values.append(arg)
            specs.append(
                smem if arg.dtype == jnp.int32 else pl.BlockSpec(arg.shape, lambda i, n=arg.ndim: (0,) * n)
            )
    single = not isinstance(outs, (list, tuple))
    shapes = [outs] if single else list(outs)
    got = pl.pallas_call(
        kernel,
        out_shape=shapes,
        in_specs=specs,
        out_specs=[pl.BlockSpec(s.shape, lambda i, n=len(s.shape): (0,) * n) for s in shapes],
        grid=(1,),
        cost_estimate=pl.CostEstimate(flops=flops, bytes_accessed=moved, transcendentals=0),
        compiler_params=pltpu.CompilerParams(vmem_limit_bytes=32 << 20),
        name=name,
    )(*values)
    return got[0] if single else got


def halved(value, bit, stride):
    half = value.shape[1] // 2
    pair = value.reshape(value.shape[0], 2, half, value.shape[2])
    low, high = pair[:, 0], pair[:, 1]
    keep = jnp.where(bit, high, low)
    send = jnp.where(bit, low, high)
    got = swapped(send, "tok", stride)
    return (keep.astype(F32) + got.astype(F32)).astype(BF16)


def doubled(value, bit, stride):
    got = swapped(value, "tok", stride)
    low = jnp.where(bit, got, value)
    high = jnp.where(bit, value, got)
    return jnp.concatenate([low, high], axis=1)


def on_device(tokens, cotangent, weights, pattern, owners, lat_in, lat_out):
    rows, chans = tokens.shape
    blk = weights.shape[-1]
    count = rows // blk
    levels = weights.shape[1]
    groups = lax.axis_size("grp")
    ranks = lax.axis_size("tok")
    assert weights.shape[2] == count
    parts = CHUNKS if chans % (CHUNKS * 128) == 0 else 1
    width = chans // parts
    chunk = jax.ShapeDtypeStruct((rows, width), BF16)
    chunk32 = jax.ShapeDtypeStruct((rows, width), F32)
    whole = jax.ShapeDtypeStruct((rows, chans), BF16)
    mac = 2 * rows * rows * width
    piece = 2 * rows * width
    wbytes = 2 * count * count * blk * blk

    def level_weights(lev):
        spec = pl.BlockSpec((count, 1, count, blk, blk), lambda i: (0, lev, 0, 0, 0))
        return (weights, spec)

    def column(array, c):
        return (array, pl.BlockSpec((rows, width), lambda i: (0, c)))

    me = lax.axis_index("tok")
    bits = [((me >> i) & 1) == 1 for i in range(levels - 1)]

    current = call(
        functools.partial(first_kernel, count, blk, width),
        [chunk] * parts,
        "first",
        mac * parts,
        2 * piece * parts + wbytes,
        pattern,
        tokens,
        level_weights(0),
    )
    lat = jnp.stack(
        [
            jnp.einsum("tr,tc->rc", lat_in, tokens, preferred_element_type=F32),
            jnp.einsum("tr,tc->rc", lat_out, cotangent, preferred_element_type=F32),
        ]
    ).astype(BF16)
    sources = [[column(tokens, c) for c in range(parts)]]
    acts = [None] * parts
    grads = [None] * parts
    backs = [None] * parts
    for lev in range(1, levels):
        arrived = [swapped(current[c], "tok", lev - 1) for c in range(parts)]
        lat = halved(lat, bits[lev - 1], lev - 1)
        sources.append(arrived)
        if lev < levels - 1:
            current = [
                call(
                    functools.partial(forward_kernel, count, blk, lev),
                    chunk,
                    "fwd",
                    mac,
                    3 * piece + wbytes,
                    pattern,
                    current[c],
                    arrived[c],
                    level_weights(lev),
                )
                for c in range(parts)
            ]
        else:
            for c in range(parts):
                acts[c], grads[c], backs[c] = call(
                    functools.partial(turn_kernel, count, blk, lev),
                    [chunk32, chunk, chunk],
                    "turn",
                    2 * mac,
                    7 * piece + wbytes,
                    pattern,
                    current[c],
                    arrived[c],
                    column(cotangent, c),
                    level_weights(lev),
                )
    block_grads = [None] * levels

    def weight_grad(lev):
        block_grads[lev] = call(
            functools.partial(weight_kernel, count, blk, lev, parts),
            jax.ShapeDtypeStruct((count * count, blk, blk), BF16),
            "wgrad",
            mac * parts,
            2 * piece * parts + wbytes,
            pattern,
            *grads,
            *sources[lev],
        )

    chains = [None] * parts
    for lev in reversed(range(1, levels)):
        arrived = [swapped(backs[c], "tok", lev - 1) for c in range(parts)]
        weight_grad(lev)
        lat = doubled(lat, bits[lev - 1], lev - 1)
        for c in range(parts):
            if lev > 1:
                grads[c], backs[c] = call(
                    functools.partial(backward_kernel, count, blk, lev - 1),
                    [chunk, chunk],
                    "bwd",
                    mac,
                    4 * piece + wbytes,
                    pattern,
                    grads[c],
                    arrived[c],
                    level_weights(lev - 1),
                )
            else:
                grads[c], chains[c] = call(
                    functools.partial(base_kernel, count, blk),
                    [chunk, chunk32],
                    "base",
                    mac,
                    5 * piece + wbytes,
                    pattern,
                    grads[c],
                    arrived[c],
                    level_weights(0),
                )
    weight_grad(0)

    def finish(array, small, terms):
        return call(
            functools.partial(latent_kernel, width, parts),
            whole,
            "latent",
            2 * rows * array.shape[1] * chans,
            3 * piece * parts,
            array,
            small,
            *terms,
        )

    mixed = finish(lat_out, lat[0], acts)
    grad_tokens = finish(lat_in, lat[1], chains)

    nblk = levels * count * count
    most = min(nblk, 2 * nblk // groups)
    if groups == 2:
        theirs = [lax.ppermute(g, "grp", [(0, 1), (1, 0)]) for g in block_grads]
        grad_blocks = call(
            functools.partial(place_kernel, count, levels),
            jax.ShapeDtypeStruct((most, blk, blk), BF16),
            "place",
            0,
            3 * 2 * nblk * blk * blk,
            owners,
            lax.axis_index("grp").astype(jnp.int32).reshape(1),
            *block_grads,
            *theirs,
        )
    else:
        partial_grads = jnp.stack(
            [g.reshape(count, count, blk, blk) for g in block_grads], axis=1
        ).reshape(nblk, blk, blk)
        own = owners[:, 0]
        marks = (own[:, None] == jnp.arange(groups, dtype=jnp.int32)).astype(jnp.int32)
        order = jnp.cumsum(marks, axis=0) - marks
        slots = jnp.sum(order * marks, axis=1)
        outbox = jnp.zeros((groups * most, blk, blk), BF16).at[own * most + slots].set(partial_grads)
        grad_blocks = lax.psum_scatter(outbox, "grp", scatter_dimension=0, tiled=True)
    return (mixed, grad_tokens, grad_blocks)


def solution(mesh):
    return jax.shard_map(
        on_device,
        mesh=mesh,
        in_specs=(
            P("tok", "grp"),
            P("tok", "grp"),
            P("tok", None, None, None, None),
            P("tok", None, None),
            P("tok", None),
            P("tok", None),
            P("tok", None),
        ),
        out_specs=(P("tok", "grp"), P("tok", "grp"), P(("tok", "grp"), None, None)),
        check_vma=False,
    )
```
